32 devices in a mesh: dp: 4 (over y, x), ctx: 2 (over core), tp: 4 (over z).
Axes of the slice: x: 2, y: 2, z: 4, core: 2. Of those that a mesh axis runs over, the one named last changes fastest.
Arguments:
- block_input_activations: bfloat16 [8192, 1024], P(('dp', 'ctx')), may hold values from -6 to 6
- sequence_first_token: int32 [8192], P(('dp', 'ctx')), may hold values from 0 to 1, as said below
- norm_gain: float32 [1024], replicated, may hold values from 0.5 to 1.5
- gate_proj: bfloat16 [1024, 2048], P(('dp', 'ctx'), 'tp'), may hold values from -0.1875 to 0.1875
- input_proj: bfloat16 [1024, 2048], P(('dp', 'ctx'), 'tp'), may hold values from -0.1875 to 0.1875
- step_proj: bfloat16 [1024, 32], P(('dp', 'ctx'), 'tp'), may hold values from -0.1875 to 0.1875
- state_proj: bfloat16 [1024, 256], P(('dp', 'ctx')), may hold values from -0.1875 to 0.1875
- conv_inner_weight: float32 [4, 2048], P(None, 'tp'), may hold values from -3 to 3
- conv_inner_bias: float32 [2048], P('tp'), may hold values from -0.5 to 0.5
- conv_state_weight: float32 [4, 256], replicated, may hold values from -3 to 3
- conv_state_bias: float32 [256], replicated, may hold values from -0.5 to 0.5
- step_bias: float32 [32], P('tp'), may hold values from -6 to -2
- decay_log: float32 [32], P('tp'), may hold values from 0 to 2.5
- skip_weight: float32 [32], P('tp'), may hold values from 0.5 to 1.5
- gate_gain: float32 [2048], P('tp'), may hold values from 0.5 to 1.5
- out_proj: bfloat16 [2048, 1024], P('tp', ('dp', 'ctx')), may hold values from -0.125 to 0.125
- output_cotangent: bfloat16 [8192, 1024], P(('dp', 'ctx')), may hold values from -6 to 6
Outputs:
- block_output: bfloat16 [8192, 1024], P(('dp', 'ctx'), 'tp')
- input_grad: float32 [8192, 1024], P(('dp', 'ctx'), 'tp')
- norm_gain_grad: float32 [1024], P('tp')
- gate_proj_grad: float32 [1024, 2048], P(('dp', 'ctx'), 'tp')
- input_proj_grad: float32 [1024, 2048], P(('dp', 'ctx'), 'tp')
- step_proj_grad: float32 [1024, 32], P(('dp', 'ctx'), 'tp')
- state_proj_grad: float32 [1024, 256], P(('dp', 'ctx'))
- conv_inner_weight_grad: float32 [4, 2048], P(None, 'tp')
- conv_inner_bias_grad: float32 [2048], P('tp')
- conv_state_weight_grad: float32 [4, 256], replicated
- conv_state_bias_grad: float32 [256], replicated
- step_bias_grad: float32 [32], P('tp')
- decay_log_grad: float32 [32], P('tp')
- skip_weight_grad: float32 [32], P('tp')
- gate_gain_grad: float32 [2048], P('tp')
- out_proj_grad: float32 [2048, 1024], P('tp', ('dp', 'ctx'))
The draws below stay inside these ranges and needn't reach their ends.
Inputs may be any that keep to these rules, and one draw needn't show every extreme that they name: `sequence_first_token`: every packed row of 2048 tokens begins with a 1; every sequence has 1 to 1536 positions, and each row holds one of exactly 1536.
All inputs are finite; a program needn't handle non-finite values.
Results may differ from the reference program's by a relative error of at most 0.012.
Values may be sent and summed in bfloat16 or wider, within the bound.
A program may use at most 128 MiB of HBM per device.

```python
import jax
import jax.numpy as jnp
from jax import lax

MODEL_WIDTH = 1024
HEADS = 32
HEADDIM = 64
STATE = 128
KCONV = 4
SPAN = 256
INNER = 2048
ROW_POSITIONS = 2048
LONGEST_SEQUENCE = 1536
PACKED_ROWS = 4
TOKENS = 8192


def draw_sequence_first_token(key, part):
    offset_random_key = jax.random.fold_in(key, 11)
    random_key_base = jax.random.fold_in(key, 23)
    start_shifts = jax.random.randint(offset_random_key, (PACKED_ROWS,), 1, ROW_POSITIONS - LONGEST_SEQUENCE + 1)
    token_position = jnp.arange(ROW_POSITIONS)
    relative = token_position[None, :] - start_shifts[:, None]
    long_start = relative == 0
    long_end = relative == LONGEST_SEQUENCE
    inside = (relative > 0) & (relative < LONGEST_SEQUENCE)
    sampled_starts = jax.random.randint(random_key_base, (PACKED_ROWS, ROW_POSITIONS), 0, 48) == 0
    sequence_starts = long_start | long_end | sampled_starts & jnp.logical_not(inside) | (token_position[None, :] == 0)
    return sequence_starts.astype(jnp.int32).reshape(PACKED_ROWS * ROW_POSITIONS)


def block_levels(own_key, dims, shards, least, top_value):
    level = 1.0
    for axis_at, blocks in shards:
        steps = jax.random.uniform(jax.random.fold_in(jax.random.fold_in(own_key, 6), axis_at), (blocks,), jnp.float32, least / len(shards), top_value / len(shards))
        level = level * jnp.repeat(jnp.exp(steps), dims[axis_at] // blocks).reshape((-1,) + (1,) * (len(dims) - 1 - axis_at))
    return level


def normal_values(rng, shape, scale, bound, cuts=(), kind=jnp.bfloat16):
    drawn = scale * jax.random.normal(rng, shape, jnp.float32)
    if cuts:
        drawn = drawn * block_levels(rng, shape, cuts, -0.22, 0.18)
    return jnp.clip(drawn, -bound, bound).astype(kind)


def setup_inputs(seed: int = 0) -> dict:
    splits = jax.random.split(jax.random.key(seed), 18)
    return {
        "block_input_activations": normal_values(splits[0], (TOKENS, MODEL_WIDTH), 1.0, 6.0, ((0, 8),)),
        "sequence_first_token": draw_sequence_first_token(jax.random.fold_in(splits[17], 71), 0),
        "norm_gain": jnp.clip(1.0 + 0.1 * jax.random.normal(splits[2], (MODEL_WIDTH,), jnp.float32), 0.5, 1.5),
        "gate_proj": normal_values(splits[3], (MODEL_WIDTH, INNER), MODEL_WIDTH ** -0.5, 0.1875, ((0, 8), (1, 4))),
        "input_proj": normal_values(splits[4], (MODEL_WIDTH, INNER), MODEL_WIDTH ** -0.5, 0.1875, ((0, 8), (1, 4))),
        "step_proj": normal_values(splits[5], (MODEL_WIDTH, HEADS), MODEL_WIDTH ** -0.5, 0.1875, ((0, 8), (1, 4))),
        "state_proj": normal_values(splits[6], (MODEL_WIDTH, 2 * STATE), MODEL_WIDTH ** -0.5, 0.1875, ((0, 8),)),
        "conv_inner_weight": normal_values(splits[7], (KCONV, INNER), KCONV ** -0.5, 3.0, ((1, 4),), jnp.float32),
        "conv_inner_bias": jnp.clip(jax.random.uniform(splits[8], (INNER,), jnp.float32, -0.5, 0.5) * block_levels(splits[8], (INNER,), ((0, 4),), -0.4, 0.0), -0.5, 0.5),
        "conv_state_weight": normal_values(splits[9], (KCONV, 2 * STATE), KCONV ** -0.5, 3.0, (), jnp.float32),
        "conv_state_bias": jnp.clip(jax.random.uniform(splits[10], (2 * STATE,), jnp.float32, -0.5, 0.5), -0.5, 0.5),
        "step_bias": jnp.clip(-6.0 + 4.0 * jax.random.uniform(splits[11], (HEADS,), jnp.float32) ** block_levels(splits[11], (HEADS,), ((0, 4),), -0.2, 0.2), -6.0, -2.0),
        "decay_log": jnp.clip(2.5 * jax.random.uniform(splits[12], (HEADS,), jnp.float32) ** block_levels(splits[12], (HEADS,), ((0, 4),), -0.2, 0.2), 0.0, 2.5),
        "skip_weight": jnp.clip(0.5 + 1.0 * jax.random.uniform(splits[13], (HEADS,), jnp.float32) ** block_levels(splits[13], (HEADS,), ((0, 4),), -0.2, 0.2), 0.5, 1.5),
        "gate_gain": jnp.clip(1.0 + 0.1 * jax.random.normal(splits[14], (INNER,), jnp.float32), 0.5, 1.5),
        "out_proj": normal_values(splits[15], (INNER, MODEL_WIDTH), INNER ** -0.5, 0.125, ((0, 4), (1, 8))),
        "output_cotangent": normal_values(splits[16], (TOKENS, MODEL_WIDTH), 1.0, 6.0, ((0, 8),)),
    }


EPSILON = 1e-05
HIGHEST = lax.Precision.HIGHEST

def conv_apply(padded, flags_padded, conv_weight, conv_bias):
    width = KCONV - 1
    count = padded.shape[0] - width
    segments = jnp.cumsum(flags_padded)
    own = segments[width:]
    result = jnp.zeros((count, padded.shape[1]), jnp.float32) + conv_bias[None, :]
    for lag in range(KCONV):
        valid = (segments[width - lag:width - lag + count] == own).astype(jnp.float32)
        result = result + conv_weight[lag][None, :] * padded[width - lag:width - lag + count] * valid[:, None]
    return result

def span_parts(inner_values, step_size, state_in, state_out, sequence_starts, decay_rate):
    count = inner_values.shape[0]
    heads = step_size.shape[1]
    spans = count // SPAN
    log_decay = (step_size * decay_rate[None, :]).reshape(spans, SPAN, heads)
    cumulative = jnp.cumsum(log_decay, axis=1)
    segments = jnp.cumsum(sequence_starts.reshape(spans, SPAN), axis=1)
    block_values = inner_values.reshape(spans, SPAN, heads, HEADDIM)
    block_step = step_size.reshape(spans, SPAN, heads)
    block_in = state_in.reshape(spans, SPAN, STATE)
    block_out = state_out.reshape(spans, SPAN, STATE)
    order = jnp.arange(SPAN)
    lower = order[:, None] >= order[None, :]
    same = ((segments[:, :, None] == segments[:, None, :]) & lower[None])[..., None]
    spread = cumulative[:, :, None, :] - cumulative[:, None, :, :]
    decay = jnp.where(same, jnp.exp(jnp.where(same, spread, 0.0)), 0.0)
    scores = jnp.einsum('ktn,ksn->kts', block_out, block_in, precision=HIGHEST)
    mixing = decay * scores[..., None] * block_step[:, None, :, :]
    inner_mixed = jnp.einsum('ktsh,kshp->kthp', mixing, block_values, precision=HIGHEST)
    ending = (segments == segments[:, -1:])[..., None]
    to_end = jnp.where(ending, jnp.exp(cumulative[:, -1:, :] - cumulative), 0.0) * block_step
    states = jnp.einsum('kshp,ksn->khpn', block_values * to_end[..., None], block_in, precision=HIGHEST)
    passing = jnp.where((segments == 0)[..., None], jnp.exp(cumulative), 0.0)
    return (inner_mixed, states, passing)

def fold_spans(states, passing):
    ends = passing[:, -1, :]

    def advance(carry, item):
        zero_state, product = carry
        state, end = item
        return ((end[:, None, None] * zero_state + state, end * product), (zero_state, product))
    init = (jnp.zeros(states.shape[1:], jnp.float32), jnp.ones(ends.shape[1:], jnp.float32))
    (final_state, final_product), (span_states, span_decays) = lax.scan(advance, init, (states, ends))
    return (span_states, span_decays, final_state, final_product)

def mixer_front(padded, flags_padded, sequence_starts, step_raw, conv_weight, conv_bias, step_bias, decay_log):
    inner_width = padded.shape[1] - 2 * STATE
    activated = jax.nn.silu(conv_apply(padded, flags_padded, conv_weight, conv_bias))
    inner_values = activated[:, :inner_width]
    state_in = activated[:, inner_width:inner_width + STATE]
    state_out = activated[:, inner_width + STATE:]
    step_size = jax.nn.softplus(step_raw + step_bias[None, :])
    decay_rate = -jnp.exp(decay_log)
    inner_mixed, states, passing = span_parts(inner_values, step_size, state_in, state_out, sequence_starts, decay_rate)
    span_states, span_decays, final_state, final_product = fold_spans(states, passing)
    kept = (inner_values, state_out, inner_mixed, passing, span_states, span_decays)
    return (kept, final_state, final_product)

def finish(kept, carried, skip):
    inner_values, state_out, inner_mixed, passing, span_states, span_decays = kept
    spans = inner_mixed.shape[0]
    heads = inner_mixed.shape[2]
    initial = span_states + span_decays[:, :, None, None] * carried[None]
    block_out = state_out.reshape(spans, SPAN, STATE)
    from_state = jnp.einsum('ktn,khpn->kthp', block_out, initial, precision=HIGHEST)
    block_values = inner_values.reshape(spans, SPAN, heads, HEADDIM)
    total = inner_mixed + passing[..., None] * from_state + skip[None, None, :, None] * block_values
    return total.reshape(inner_values.shape[0], heads * HEADDIM)

def mixer(padded, flags_padded, sequence_starts, step_raw, conv_weight, conv_bias, step_bias, decay_log, skip, carried):
    kept, final_state, final_product = mixer_front(padded, flags_padded, sequence_starts, step_raw, conv_weight, conv_bias, step_bias, decay_log)
    output = finish(kept, carried, skip)
    return (output, final_state + final_product[:, None, None] * carried)

def reference(block_input_activations, sequence_first_token, norm_gain, gate_proj, input_proj, step_proj, state_proj, conv_inner_weight, conv_inner_bias, conv_state_weight, conv_state_bias, step_bias, decay_log, skip_weight, gate_gain, out_proj, output_cotangent):
    main_weight = jnp.concatenate([gate_proj, input_proj, state_proj], axis=1)
    conv_weight = jnp.concatenate([conv_inner_weight, conv_state_weight], axis=1)
    conv_bias = jnp.concatenate([conv_inner_bias, conv_state_bias])
    width = KCONV - 1
    carried_zero = jnp.zeros((HEADS, HEADDIM, STATE), jnp.float32)

    def row_pass(totals, item):
        input_row, start_row, cotangent_row = item
        hidden = input_row.astype(jnp.float32)
        inv_rms = lax.rsqrt(lax.optimization_barrier(jnp.mean(hidden * hidden, axis=1, keepdims=True)) + EPSILON)
        normed = (hidden * inv_rms * norm_gain[None, :]).astype(jnp.bfloat16)
        projected = jnp.dot(normed, main_weight, preferred_element_type=jnp.float32)
        step_raw = jnp.dot(normed, step_proj, preferred_element_type=jnp.float32)
        gate = projected[:, :INNER]
        conv_rows = projected[:, INNER:].astype(jnp.bfloat16)
        sequence_starts = start_row.astype(jnp.float32)
        padded = jnp.concatenate([jnp.zeros((width, INNER + 2 * STATE), jnp.float32), conv_rows.astype(jnp.float32)], axis=0)
        flags_padded = jnp.concatenate([jnp.zeros((width,), jnp.float32), sequence_starts])

        def local_mixer(padded_in, raw_in, weight_in, bias_in, step_in, decay_in, skip_in):
            return mixer(padded_in, flags_padded, sequence_starts, raw_in, weight_in, bias_in, step_in, decay_in, skip_in, carried_zero)[0]
        mixed, pullback = jax.vjp(local_mixer, padded, step_raw, conv_weight, conv_bias, step_bias, decay_log, skip_weight)
        gate_silu = jax.nn.silu(gate)
        gated = mixed * gate_silu
        gate_inv = lax.rsqrt(lax.optimization_barrier(jnp.mean(gated * gated, axis=1, keepdims=True)) + EPSILON)
        gated_normed = (gated * gate_inv * gate_gain[None, :]).astype(jnp.bfloat16)
        branch = jnp.dot(gated_normed, out_proj, preferred_element_type=jnp.float32)
        output_row = (hidden + branch).astype(jnp.bfloat16)
        grad_gated_normed = jnp.dot(cotangent_row, out_proj.T, preferred_element_type=jnp.float32)
        grad_out = jnp.dot(gated_normed.T, cotangent_row, preferred_element_type=jnp.float32)
        scaled = grad_gated_normed * gate_gain[None, :]
        grad_gated = gate_inv * scaled - gated * gate_inv ** 3 * lax.optimization_barrier(jnp.mean(gated * scaled, axis=1, keepdims=True))
        grad_gain_gate = lax.optimization_barrier(jnp.sum(grad_gated_normed * gated * gate_inv, axis=0))
        sigmoid_gate = jax.nn.sigmoid(gate)
        grad_mixed = grad_gated * gate_silu
        grad_gate = grad_gated * mixed * sigmoid_gate * (1.0 + gate * (1.0 - sigmoid_gate))
        grad_padded, grad_step_raw, grad_conv_weight, grad_conv_bias, grad_step_bias, grad_decay_log, grad_skip = pullback(grad_mixed)
        grad_main = jnp.concatenate([grad_gate, grad_padded[width:]], axis=1).astype(jnp.bfloat16)
        grad_step = grad_step_raw.astype(jnp.bfloat16)
        grad_main_weight = jnp.dot(normed.T, grad_main, preferred_element_type=jnp.float32)
        grad_step_weight = jnp.dot(normed.T, grad_step, preferred_element_type=jnp.float32)
        grad_normed = jnp.dot(grad_main, main_weight.T, preferred_element_type=jnp.float32) + jnp.dot(grad_step, step_proj.T, preferred_element_type=jnp.float32)
        scaled_in = grad_normed * norm_gain[None, :]
        grad_row = cotangent_row.astype(jnp.float32) + inv_rms * scaled_in - hidden * inv_rms ** 3 * lax.optimization_barrier(jnp.mean(hidden * scaled_in, axis=1, keepdims=True))
        grad_gain_norm = lax.optimization_barrier(jnp.sum(grad_normed * hidden * inv_rms, axis=0))
        terms = (grad_main_weight, grad_step_weight, grad_out, grad_conv_weight, grad_conv_bias, grad_step_bias, grad_decay_log, grad_skip, grad_gain_gate, grad_gain_norm)
        return (jax.tree.map(lambda first, second: first + second, totals, terms), (output_row, grad_row))
    init = (jnp.zeros((MODEL_WIDTH, 2 * INNER + 2 * STATE), jnp.float32), jnp.zeros((MODEL_WIDTH, HEADS), jnp.float32), jnp.zeros((INNER, MODEL_WIDTH), jnp.float32), jnp.zeros((KCONV, INNER + 2 * STATE), jnp.float32), jnp.zeros((INNER + 2 * STATE,), jnp.float32), jnp.zeros((HEADS,), jnp.float32), jnp.zeros((HEADS,), jnp.float32), jnp.zeros((HEADS,), jnp.float32), jnp.zeros((INNER,), jnp.float32), jnp.zeros((MODEL_WIDTH,), jnp.float32))
    entry_list = (block_input_activations.reshape(PACKED_ROWS, ROW_POSITIONS, MODEL_WIDTH), sequence_first_token.reshape(PACKED_ROWS, ROW_POSITIONS), output_cotangent.reshape(PACKED_ROWS, ROW_POSITIONS, MODEL_WIDTH))
    totals, (output_rows, grad_rows) = lax.scan(row_pass, init, entry_list)
    grad_main_weight, grad_step_weight, grad_out, grad_conv_weight, grad_conv_bias, grad_step_bias, grad_decay_log, grad_skip, grad_gain_gate, grad_gain_norm = totals
    return (output_rows.reshape(TOKENS, MODEL_WIDTH), grad_rows.reshape(TOKENS, MODEL_WIDTH), grad_gain_norm, grad_main_weight[:, :INNER], grad_main_weight[:, INNER:2 * INNER], grad_step_weight, grad_main_weight[:, 2 * INNER:], grad_conv_weight[:, :INNER], grad_conv_bias[:INNER], grad_conv_weight[:, INNER:], grad_conv_bias[INNER:], grad_step_bias, grad_decay_log, grad_skip, grad_gain_gate, grad_out)
```

```python
import jax
import jax.numpy as jnp
from jax import lax
from jax.sharding import PartitionSpec as P

MODEL_WIDTH = 1024
HEADDIM = 64
STATE = 128
KCONV = 4
SPAN = 256
INNER = 2048


EPSILON = 1e-05
HIGHEST = lax.Precision.HIGHEST


def passed_along(block, distance):
    devices = range(lax.axis_size("ctx"))
    route = [(i - distance, i) for i in devices if i - distance in devices]
    return lax.ppermute(block, "ctx", route)


def conv_apply(padded, flags_padded, conv_weight, conv_bias):
    width = KCONV - 1
    count = padded.shape[0] - width
    segments = jnp.cumsum(flags_padded)
    own = segments[width:]
    result = jnp.zeros((count, padded.shape[1]), jnp.float32) + conv_bias[None, :]
    for lag in range(KCONV):
        valid = (segments[width - lag : width - lag + count] == own).astype(jnp.float32)
        result = (
            result
            + conv_weight[lag][None, :] * padded[width - lag : width - lag + count] * valid[:, None]
        )
    return result


def span_parts(inner_values, step_size, state_in, state_out, sequence_starts, decay_rate):
    count = inner_values.shape[0]
    heads = step_size.shape[1]
    spans = count // SPAN
    log_decay = (step_size * decay_rate[None, :]).reshape(spans, SPAN, heads)
    ones_below = jnp.tril(jnp.ones((SPAN, SPAN), jnp.float32))
    cumulative = jnp.einsum("ts,ksh->kth", ones_below, log_decay, precision=HIGHEST)
    segments = jnp.cumsum(sequence_starts.reshape(spans, SPAN), axis=1)
    block_values = inner_values.reshape(spans, SPAN, heads, HEADDIM)
    block_step = step_size.reshape(spans, SPAN, heads)
    block_in = state_in.reshape(spans, SPAN, STATE)
    block_out = state_out.reshape(spans, SPAN, STATE)
    order = jnp.arange(SPAN)
    lower = order[:, None] >= order[None, :]
    same = ((segments[:, :, None] == segments[:, None, :]) & lower[None])[..., None]
    spread = cumulative[:, :, None, :] - cumulative[:, None, :, :]
    decay = jnp.where(same, jnp.exp(jnp.where(same, spread, 0.0)), 0.0)
    scores = jnp.einsum("ktn,ksn->kts", block_out, block_in)
    mixing = decay * scores[..., None] * block_step[:, None, :, :]
    inner_mixed = jnp.einsum("ktsh,kshp->kthp", mixing, block_values)
    ending = (segments == segments[:, -1:])[..., None]
    to_end = jnp.where(ending, jnp.exp(cumulative[:, -1:, :] - cumulative), 0.0) * block_step
    states = jnp.einsum(
        "kshp,ksn->khpn", block_values * to_end[..., None], block_in
    )
    passing = jnp.where((segments == 0)[..., None], jnp.exp(cumulative), 0.0)
    return (inner_mixed, states, passing)


def fold_spans(states, passing):
    ends = passing[:, -1, :]
    state = jnp.zeros(states.shape[1:], jnp.float32)
    product = jnp.ones(ends.shape[1:], jnp.float32)
    span_states, span_decays = [], []
    for k in range(states.shape[0]):
        span_states.append(state)
        span_decays.append(product)
        state = ends[k][:, None, None] * state + states[k]
        product = ends[k] * product
    return (jnp.stack(span_states), jnp.stack(span_decays), state, product)


def mixer_front(
    padded, flags_padded, sequence_starts, step_raw, conv_weight, conv_bias, step_bias, decay_log
):
    inner_width = padded.shape[1] - 2 * STATE
    activated = jax.nn.silu(conv_apply(padded, flags_padded, conv_weight, conv_bias))
    inner_values = activated[:, :inner_width]
    state_in = activated[:, inner_width : inner_width + STATE]
    state_out = activated[:, inner_width + STATE :]
    step_size = jax.nn.softplus(step_raw + step_bias[None, :])
    decay_rate = -jnp.exp(decay_log)
    inner_mixed, states, passing = span_parts(
        inner_values, step_size, state_in, state_out, sequence_starts, decay_rate
    )
    span_states, span_decays, final_state, final_product = fold_spans(states, passing)
    kept = (inner_values, state_out, inner_mixed, passing, span_states, span_decays)
    return (kept, final_state, final_product)


def finish(kept, carried, skip):
    inner_values, state_out, inner_mixed, passing, span_states, span_decays = kept
    spans = inner_mixed.shape[0]
    heads = inner_mixed.shape[2]
    initial = span_states + span_decays[:, :, None, None] * carried[None]
    block_out = state_out.reshape(spans, SPAN, STATE)
    from_state = jnp.einsum("ktn,khpn->kthp", block_out, initial)
    block_values = inner_values.reshape(spans, SPAN, heads, HEADDIM)
    total = inner_mixed + passing[..., None] * from_state + skip[None, None, :, None] * block_values
    return total.reshape(inner_values.shape[0], heads * HEADDIM)


def mixer(
    padded,
    flags_padded,
    sequence_starts,
    step_raw,
    conv_weight,
    conv_bias,
    step_bias,
    decay_log,
    skip,
    carried,
):
    kept, final_state, final_product = mixer_front(
        padded,
        flags_padded,
        sequence_starts,
        step_raw,
        conv_weight,
        conv_bias,
        step_bias,
        decay_log,
    )
    output = finish(kept, carried, skip)
    return (output, final_state + final_product[:, None, None] * carried)


def on_device(
    block_input_activations,
    sequence_first_token,
    norm_gain,
    gate_proj,
    input_proj,
    step_proj,
    state_proj,
    conv_inner_weight,
    conv_inner_bias,
    conv_state_weight,
    conv_state_bias,
    step_bias,
    decay_log,
    skip_weight,
    gate_gain,
    out_proj,
    output_cotangent,
):
    everyone = ("dp", "ctx")
    bf16 = jnp.bfloat16
    local_inner = gate_proj.shape[1]
    heads = step_bias.shape[0]
    width = KCONV - 1
    full_weight = lax.all_gather(
        jnp.concatenate([gate_proj, input_proj, state_proj, step_proj], axis=1),
        everyone,
        axis=0,
        tiled=True,
    )
    full_out_t = lax.all_gather(out_proj.T, everyone, axis=0, tiled=True)
    hidden = block_input_activations.astype(jnp.float32)
    inv_rms = lax.rsqrt(jnp.mean(hidden * hidden, axis=1, keepdims=True) + EPSILON)
    normed = (hidden * inv_rms * norm_gain[None, :]).astype(bf16)
    projected = jnp.dot(normed, full_weight, preferred_element_type=jnp.float32)
    step_raw = projected[:, 2 * local_inner + 2 * STATE :]
    gate = projected[:, :local_inner]
    conv_rows = projected[:, local_inner : 2 * local_inner + 2 * STATE].astype(bf16)
    sequence_starts = sequence_first_token.astype(jnp.float32)
    tail_rows, tail_flags = passed_along(
        (conv_rows[-width:], sequence_starts[-width:].astype(bf16)), 1
    )
    padded = jnp.concatenate([tail_rows, conv_rows], axis=0).astype(jnp.float32)
    flags_padded = jnp.concatenate([tail_flags.astype(jnp.float32), sequence_starts])
    conv_weight = jnp.concatenate([conv_inner_weight, conv_state_weight], axis=1)
    conv_bias = jnp.concatenate([conv_inner_bias, conv_state_bias])
    kept, final_state, final_product = mixer_front(
        padded,
        flags_padded,
        sequence_starts,
        step_raw,
        conv_weight,
        conv_bias,
        step_bias,
        decay_log,
    )
    carried = passed_along(final_state, 1)
    mixed = finish(kept, carried, skip_weight)
    gate_silu = jax.nn.silu(gate)
    gated = mixed * gate_silu
    grad_gated_normed = jnp.dot(output_cotangent, full_out_t, preferred_element_type=jnp.float32)
    scaled = grad_gated_normed * gate_gain[None, :]
    row_sums = lax.psum(
        jnp.stack([jnp.sum(gated * gated, axis=1), jnp.sum(gated * scaled, axis=1)]), "tp"
    )
    gate_inv = lax.rsqrt(row_sums[0] / INNER + EPSILON)[:, None]
    gated_normed = (gated * gate_inv * gate_gain[None, :]).astype(bf16)
    share = MODEL_WIDTH // lax.axis_size("tp")
    column = lax.axis_index("tp") * share
    branch = lax.psum_scatter(
        lax.dot_general(
            gated_normed, full_out_t, (((1,), (1,)), ((), ())), preferred_element_type=jnp.float32
        ).astype(bf16),
        "tp",
        scatter_dimension=1,
        tiled=True,
    )
    own_hidden = lax.dynamic_slice_in_dim(hidden, column, share, 1)
    block_output = (own_hidden + branch.astype(jnp.float32)).astype(bf16)
    grad_gated = gate_inv * scaled - gated * gate_inv**3 * (row_sums[1] / INNER)[:, None]
    grad_gain_gate = jnp.sum(grad_gated_normed * gated * gate_inv, axis=0)
    sigmoid_gate = jax.nn.sigmoid(gate)
    grad_mixed = grad_gated * gate_silu
    grad_gate = (
        grad_gated * mixed * sigmoid_gate * (1.0 + gate * (1.0 - sigmoid_gate))
    ).astype(bf16)
    grad_out = lax.dot_general(
        output_cotangent,
        gated_normed,
        (((0,), (0,)), ((), ())),
        preferred_element_type=jnp.float32,
    ).astype(bf16)
    grad_gate_weight = jnp.dot(
        normed.T, grad_gate, preferred_element_type=jnp.float32
    ).astype(bf16)
    first_grads = lax.psum_scatter(
        jnp.concatenate([grad_gate_weight, grad_out], axis=1),
        everyone,
        scatter_dimension=0,
        tiled=True,
    ).astype(jnp.float32)
    gate_grad = first_grads[:, :local_inner]
    out_proj_grad = first_grads[:, local_inner:].T

    def state_effect(carried_in):
        return finish(kept, carried_in, skip_weight)

    ignored, state_pull = jax.vjp(state_effect, carried)
    (through_mixed,) = state_pull(grad_mixed)
    next_grad = passed_along(through_mixed, -1)

    def full_mixer(padded_in, raw_in, weight_in, bias_in, step_in, decay_in, skip_in):
        return mixer(
            padded_in,
            flags_padded,
            sequence_starts,
            raw_in,
            weight_in,
            bias_in,
            step_in,
            decay_in,
            skip_in,
            carried,
        )

    ignored_out, pullback = jax.vjp(
        full_mixer,
        padded,
        step_raw,
        conv_weight,
        conv_bias,
        step_bias,
        decay_log,
        skip_weight,
    )
    (
        grad_padded,
        grad_step_raw,
        grad_conv_weight,
        grad_conv_bias,
        grad_step_bias,
        grad_decay_log,
        grad_skip,
    ) = pullback((grad_mixed, next_grad))
    returned = passed_along(grad_padded[:width], -1)
    grad_rows = grad_padded[width:]
    grad_rows = grad_rows.at[-width:].add(returned)
    grad_late = jnp.concatenate([grad_rows, grad_step_raw], axis=1).astype(bf16)
    grad_all = jnp.concatenate([grad_gate, grad_late], axis=1)
    tensor_part = lax.dot_general(
        grad_all, full_weight, (((1,), (1,)), ((), ())), preferred_element_type=jnp.float32
    )
    mean_sum = jnp.sum(hidden * norm_gain[None, :] * tensor_part, axis=1)
    own_grad = lax.psum_scatter(
        tensor_part.astype(bf16), "tp", scatter_dimension=1, tiled=True
    ).astype(jnp.float32)
    late_weight = jnp.dot(normed.T, grad_late, preferred_element_type=jnp.float32).astype(bf16)
    late_grads = lax.psum_scatter(
        late_weight, everyone, scatter_dimension=0, tiled=True
    ).astype(jnp.float32)
    mean_term = lax.psum(mean_sum, "tp")[:, None] / MODEL_WIDTH
    own_cotangent = lax.dynamic_slice_in_dim(output_cotangent, column, share, 1).astype(jnp.float32)
    own_gain = lax.dynamic_slice_in_dim(norm_gain, column, share, 0)
    input_grad = (
        own_cotangent
        + inv_rms * own_grad * own_gain[None, :]
        - own_hidden * inv_rms**3 * mean_term
    )
    grad_gain_norm = jnp.sum(own_grad * own_hidden * inv_rms, axis=0)
    parts = (
        grad_conv_weight[:, :local_inner],
        grad_conv_bias[:local_inner],
        grad_step_bias,
        grad_decay_log,
        grad_skip,
        grad_gain_gate,
        grad_gain_norm,
        grad_conv_weight[:, local_inner:],
        grad_conv_bias[local_inner:],
    )
    smalls = lax.psum(jnp.concatenate([p.reshape(-1) for p in parts]), everyone)
    split = []
    at = 0
    for p in parts:
        split.append(smalls[at : at + p.size])
        at += p.size
    state_flat = late_grads[:, local_inner : local_inner + 2 * STATE]
    shared = lax.psum(
        jnp.concatenate([split[7], split[8], state_flat.reshape(-1)]), "tp"
    )
    conv_state = shared[: KCONV * 2 * STATE].reshape(KCONV, 2 * STATE)
    bias_state = shared[KCONV * 2 * STATE : (KCONV + 1) * 2 * STATE]
    state_grad = shared[(KCONV + 1) * 2 * STATE :].reshape(state_flat.shape)
    return (
        block_output,
        input_grad,
        split[6],
        gate_grad,
        late_grads[:, :local_inner],
        late_grads[:, local_inner + 2 * STATE :],
        state_grad,
        split[0].reshape(KCONV, local_inner),
        split[1],
        conv_state,
        bias_state,
        split[2],
        split[3],
        split[4],
        split[5],
        out_proj_grad,
    )


def solution(mesh):
    return jax.shard_map(
        on_device,
        mesh=mesh,
        in_specs=(
            P(("dp", "ctx"), None),
            P(("dp", "ctx")),
            P(),
            P(("dp", "ctx"), "tp"),
            P(("dp", "ctx"), "tp"),
            P(("dp", "ctx"), "tp"),
            P(("dp", "ctx"), None),
            P(None, "tp"),
            P("tp"),
            P(),
            P(),
            P("tp"),
            P("tp"),
            P("tp"),
            P("tp"),
            P("tp", ("dp", "ctx")),
            P(("dp", "ctx"), None),
        ),
        out_specs=(
            P(("dp", "ctx"), "tp"),
            P(("dp", "ctx"), "tp"),
            P("tp"),
            P(("dp", "ctx"), "tp"),
            P(("dp", "ctx"), "tp"),
            P(("dp", "ctx"), "tp"),
            P(("dp", "ctx"), None),
            P(None, "tp"),
            P("tp"),
            P(),
            P(),
            P("tp"),
            P("tp"),
            P("tp"),
            P("tp"),
            P("tp", ("dp", "ctx")),
        ),
        check_vma=False,
    )
```

```python
import jax
import jax.numpy as jnp
from jax import lax
from jax.experimental import pallas as pl
from jax.experimental.pallas import tpu as pltpu
from jax.sharding import PartitionSpec as P

MODEL_WIDTH = 1024
HEADDIM = 64
STATE = 128
KCONV = 4
SPAN = 256
INNER = 2048


EPSILON = 1e-05
HIGHEST = lax.Precision.HIGHEST


def passed_along(block, distance):
    devices = range(lax.axis_size("ctx"))
    route = [(i - distance, i) for i in devices if i - distance in devices]
    return lax.ppermute(block, "ctx", route)


def place_in(axes):
    place = lax.axis_index(axes[0])
    for axis in axes[1:]:
        place = place * lax.axis_size(axis) + lax.axis_index(axis)
    return place


def device_at(axes, place):
    if len(axes) == 1:
        return {axes[0]: place}
    inner = lax.axis_size(axes[1])
    return {axes[0]: place // inner, axes[1]: lax.rem(place, inner)}


def exchange_kernel(plans, *refs):
    count = len(plans)
    inputs, outputs = refs[:count], refs[count : 2 * count]
    scratch = refs[2 * count :]
    greeted = []
    for axes, size, _, _ in plans:
        if axes not in greeted:
            greeted.append(axes)
    barrier = pltpu.get_barrier_semaphore()
    expected = 0
    for axes in greeted:
        size = [p[1] for p in plans if p[0] == axes][0]
        me = place_in(axes)
        for off in range(1, size):
            pl.semaphore_signal(
                barrier,
                inc=1,
                device_id=device_at(axes, lax.rem(me + off, size)),
                device_id_type=pl.DeviceIdType.MESH,
            )
        expected += size - 1
    pl.semaphore_wait(barrier, expected)
    copies = []
    for index, (axes, size, dim, block) in enumerate(plans):
        received, own, send_sem, recv_sem, own_sem = scratch[5 * index : 5 * index + 5]
        x = inputs[index]
        me = place_in(axes)

        def piece(place, x=x, dim=dim, block=block):
            if dim is None:
                return x
            start = pl.multiple_of(place * block[dim], block[dim])
            if dim == 0:
                return x.at[pl.ds(start, block[0]), :]
            return x.at[:, pl.ds(start, block[1])]

        sends = []
        for off in range(size - 1, 0, -1):
            target = lax.rem(me + off, size)
            copy = pltpu.make_async_remote_copy(
                src_ref=piece(target),
                dst_ref=received.at[off - 1],
                send_sem=send_sem.at[off - 1],
                recv_sem=recv_sem.at[off - 1],
                device_id=device_at(axes, target),
                device_id_type=pl.DeviceIdType.MESH,
            )
            copy.start()
            sends.append(copy)
        local = pltpu.make_async_copy(piece(me), own, own_sem)
        local.start()
        copies.append((sends, local))
    for index in reversed(range(count)):
        _, size, _, block = plans[index]
        received, own = scratch[5 * index : 5 * index + 2]
        sends, local = copies[index]
        local.wait()
        for copy in sends:
            copy.wait_recv()
        rows = min(16, block[0])

        def add(step, carry, received=received, own=own, out=outputs[index], size=size, rows=rows):
            at = pl.ds(pl.multiple_of(step * rows, rows), rows)
            total = own[at, :].astype(jnp.float32)
            for k in range(size - 1):
                total = total + received[k, at, :].astype(jnp.float32)
            out[at, :] = total
            return carry

        lax.fori_loop(0, block[0] // rows, add, 0)
    for sends, _ in copies:
        for copy in sends:
            copy.wait_send()


def exchange(items, collective_id):
    plans, out_shape, scratch = [], [], []
    for x, axes, dim in items:
        size = 1
        for axis in axes:
            size *= lax.axis_size(axis)
        block = list(x.shape)
        if dim is not None:
            block[dim] //= size
        block = tuple(block)
        plans.append((axes, size, dim, block))
        out_shape.append(jax.ShapeDtypeStruct(block, jnp.float32))
        scratch += [
            pltpu.VMEM((size - 1,) + block, x.dtype),
            pltpu.VMEM(block, x.dtype),
            pltpu.SemaphoreType.DMA((size - 1,)),
            pltpu.SemaphoreType.DMA((size - 1,)),
            pltpu.SemaphoreType.DMA,
        ]
    return pl.pallas_call(
        lambda *refs: exchange_kernel(plans, *refs),
        out_shape=tuple(out_shape),
        in_specs=[pl.BlockSpec(memory_space=pl.ANY)] * len(items),
        out_specs=tuple([pl.BlockSpec(memory_space=pltpu.VMEM)] * len(items)),
        scratch_shapes=scratch,
        compiler_params=pltpu.CompilerParams(collective_id=collective_id, has_side_effects=True),
        name="exchange" + str(collective_id),
    )(*[item[0] for item in items])


def flat_rows(parts, rows):
    flat = jnp.concatenate([p.reshape(-1) for p in parts])
    return jnp.pad(flat, (0, rows * 128 - flat.shape[0])).reshape(rows, 128)


def conv_apply(padded, flags_padded, conv_weight, conv_bias):
    width = KCONV - 1
    count = padded.shape[0] - width
    segments = jnp.cumsum(flags_padded)
    own = segments[width:]
    result = jnp.zeros((count, padded.shape[1]), jnp.float32) + conv_bias[None, :]
    for lag in range(KCONV):
        valid = (segments[width - lag : width - lag + count] == own).astype(jnp.float32)
        result = (
            result
            + conv_weight[lag][None, :] * padded[width - lag : width - lag + count] * valid[:, None]
        )
    return result


def span_parts(inner_values, step_size, state_in, state_out, sequence_starts, decay_rate):
    count = inner_values.shape[0]
    heads = step_size.shape[1]
    spans = count // SPAN
    log_decay = (step_size * decay_rate[None, :]).reshape(spans, SPAN, heads)
    ones_below = jnp.tril(jnp.ones((SPAN, SPAN), jnp.float32))
    cumulative = jnp.einsum("ts,ksh->kth", ones_below, log_decay, precision=HIGHEST)
    segments = jnp.cumsum(sequence_starts.reshape(spans, SPAN), axis=1)
    block_values = inner_values.reshape(spans, SPAN, heads, HEADDIM)
    block_step = step_size.reshape(spans, SPAN, heads)
    block_in = state_in.reshape(spans, SPAN, STATE)
    block_out = state_out.reshape(spans, SPAN, STATE)
    order = jnp.arange(SPAN)
    lower = order[:, None] >= order[None, :]
    same = ((segments[:, :, None] == segments[:, None, :]) & lower[None])[..., None]
    spread = cumulative[:, :, None, :] - cumulative[:, None, :, :]
    decay = jnp.where(same, jnp.exp(jnp.where(same, spread, 0.0)), 0.0)
    scores = jnp.einsum("ktn,ksn->kts", block_out, block_in)
    mixing = decay * scores[..., None] * block_step[:, None, :, :]
    inner_mixed = jnp.einsum("ktsh,kshp->kthp", mixing, block_values)
    ending = (segments == segments[:, -1:])[..., None]
    to_end = jnp.where(ending, jnp.exp(cumulative[:, -1:, :] - cumulative), 0.0) * block_step
    states = jnp.einsum(
        "kshp,ksn->khpn", block_values * to_end[..., None], block_in
    )
    passing = jnp.where((segments == 0)[..., None], jnp.exp(cumulative), 0.0)
    return (inner_mixed, states, passing)


def fold_spans(states, passing):
    ends = passing[:, -1, :]
    state = jnp.zeros(states.shape[1:], jnp.float32)
    product = jnp.ones(ends.shape[1:], jnp.float32)
    span_states, span_decays = [], []
    for k in range(states.shape[0]):
        span_states.append(state)
        span_decays.append(product)
        state = ends[k][:, None, None] * state + states[k]
        product = ends[k] * product
    return (jnp.stack(span_states), jnp.stack(span_decays), state, product)


def mixer_front(
    padded, flags_padded, sequence_starts, step_raw, conv_weight, conv_bias, step_bias, decay_log
):
    inner_width = padded.shape[1] - 2 * STATE
    activated = jax.nn.silu(conv_apply(padded, flags_padded, conv_weight, conv_bias))
    inner_values = activated[:, :inner_width]
    state_in = activated[:, inner_width : inner_width + STATE]
    state_out = activated[:, inner_width + STATE :]
    step_size = jax.nn.softplus(step_raw + step_bias[None, :])
    decay_rate = -jnp.exp(decay_log)
    inner_mixed, states, passing = span_parts(
        inner_values, step_size, state_in, state_out, sequence_starts, decay_rate
    )
    span_states, span_decays, final_state, final_product = fold_spans(states, passing)
    kept = (inner_values, state_out, inner_mixed, passing, span_states, span_decays)
    return (kept, final_state, final_product)


def finish(kept, carried, skip):
    inner_values, state_out, inner_mixed, passing, span_states, span_decays = kept
    spans = inner_mixed.shape[0]
    heads = inner_mixed.shape[2]
    initial = span_states + span_decays[:, :, None, None] * carried[None]
    block_out = state_out.reshape(spans, SPAN, STATE)
    from_state = jnp.einsum("ktn,khpn->kthp", block_out, initial)
    block_values = inner_values.reshape(spans, SPAN, heads, HEADDIM)
    total = inner_mixed + passing[..., None] * from_state + skip[None, None, :, None] * block_values
    return total.reshape(inner_values.shape[0], heads * HEADDIM)


def mixer(
    padded,
    flags_padded,
    sequence_starts,
    step_raw,
    conv_weight,
    conv_bias,
    step_bias,
    decay_log,
    skip,
    carried,
):
    kept, final_state, final_product = mixer_front(
        padded,
        flags_padded,
        sequence_starts,
        step_raw,
        conv_weight,
        conv_bias,
        step_bias,
        decay_log,
    )
    output = finish(kept, carried, skip)
    return (output, final_state + final_product[:, None, None] * carried)


def on_device(
    block_input_activations,
    sequence_first_token,
    norm_gain,
    gate_proj,
    input_proj,
    step_proj,
    state_proj,
    conv_inner_weight,
    conv_inner_bias,
    conv_state_weight,
    conv_state_bias,
    step_bias,
    decay_log,
    skip_weight,
    gate_gain,
    out_proj,
    output_cotangent,
):
    everyone = ("dp", "ctx")
    bf16 = jnp.bfloat16
    local_inner = gate_proj.shape[1]
    heads = step_bias.shape[0]
    width = KCONV - 1
    full_weight = lax.all_gather(
        jnp.concatenate([gate_proj, input_proj, state_proj, step_proj], axis=1),
        everyone,
        axis=0,
        tiled=True,
    )
    full_out_t = lax.all_gather(out_proj.T, everyone, axis=0, tiled=True)
    hidden = block_input_activations.astype(jnp.float32)
    inv_rms = lax.rsqrt(jnp.mean(hidden * hidden, axis=1, keepdims=True) + EPSILON)
    normed = (hidden * inv_rms * norm_gain[None, :]).astype(bf16)
    projected = jnp.dot(normed, full_weight, preferred_element_type=jnp.float32)
    step_raw = projected[:, 2 * local_inner + 2 * STATE :]
    gate = projected[:, :local_inner]
    conv_rows = projected[:, local_inner : 2 * local_inner + 2 * STATE].astype(bf16)
    sequence_starts = sequence_first_token.astype(jnp.float32)
    tail_rows, tail_flags = passed_along(
        (conv_rows[-width:], sequence_starts[-width:].astype(bf16)), 1
    )
    padded = jnp.concatenate([tail_rows, conv_rows], axis=0).astype(jnp.float32)
    flags_padded = jnp.concatenate([tail_flags.astype(jnp.float32), sequence_starts])
    conv_weight = jnp.concatenate([conv_inner_weight, conv_state_weight], axis=1)
    conv_bias = jnp.concatenate([conv_inner_bias, conv_state_bias])
    kept, final_state, final_product = mixer_front(
        padded,
        flags_padded,
        sequence_starts,
        step_raw,
        conv_weight,
        conv_bias,
        step_bias,
        decay_log,
    )
    carried = passed_along(final_state, 1)
    mixed = finish(kept, carried, skip_weight)
    gate_silu = jax.nn.silu(gate)
    gated = mixed * gate_silu
    grad_gated_normed = jnp.dot(output_cotangent, full_out_t, preferred_element_type=jnp.float32)
    scaled = grad_gated_normed * gate_gain[None, :]
    tokens = hidden.shape[0]
    (row_sums,) = exchange(
        [
            (
                flat_rows(
                    [jnp.sum(gated * gated, axis=1), jnp.sum(gated * scaled, axis=1)],
                    2 * tokens // 128,
                ),
                ("tp",),
                None,
            )
        ],
        1,
    )
    row_sums = row_sums.reshape(2, tokens)
    gate_inv = lax.rsqrt(row_sums[0] / INNER + EPSILON)[:, None]
    gated_normed = (gated * gate_inv * gate_gain[None, :]).astype(bf16)
    share = MODEL_WIDTH // lax.axis_size("tp")
    column = lax.axis_index("tp") * share
    branch_part = lax.dot_general(
        gated_normed, full_out_t, (((1,), (1,)), ((), ())), preferred_element_type=jnp.float32
    ).astype(bf16)
    own_hidden = lax.dynamic_slice_in_dim(hidden, column, share, 1)
    grad_gated = gate_inv * scaled - gated * gate_inv**3 * (row_sums[1] / INNER)[:, None]
    grad_gain_gate = jnp.sum(grad_gated_normed * gated * gate_inv, axis=0)
    sigmoid_gate = jax.nn.sigmoid(gate)
    grad_mixed = grad_gated * gate_silu
    grad_gate = (
        grad_gated * mixed * sigmoid_gate * (1.0 + gate * (1.0 - sigmoid_gate))
    ).astype(bf16)
    grad_out = lax.dot_general(
        output_cotangent,
        gated_normed,
        (((0,), (0,)), ((), ())),
        preferred_element_type=jnp.float32,
    ).astype(bf16)
    grad_gate_weight = jnp.dot(
        normed.T, grad_gate, preferred_element_type=jnp.float32
    ).astype(bf16)
    first_part = jnp.concatenate([grad_gate_weight, grad_out], axis=1)
    grad_mixed, branch_part, first_part = lax.optimization_barrier(
        (grad_mixed, branch_part, first_part)
    )
    branch = lax.psum_scatter(branch_part, "tp", scatter_dimension=1, tiled=True)
    block_output = (own_hidden + branch.astype(jnp.float32)).astype(bf16)
    first_grads = lax.psum_scatter(
        first_part, everyone, scatter_dimension=0, tiled=True
    ).astype(jnp.float32)
    gate_grad = first_grads[:, :local_inner]
    out_proj_grad = first_grads[:, local_inner:].T

    def state_effect(carried_in):
        return finish(kept, carried_in, skip_weight)

    ignored, state_pull = jax.vjp(state_effect, carried)
    (through_mixed,) = state_pull(grad_mixed)
    next_grad = passed_along(through_mixed, -1)

    def full_mixer(padded_in, raw_in, weight_in, bias_in, step_in, decay_in, skip_in):
        return mixer(
            padded_in,
            flags_padded,
            sequence_starts,
            raw_in,
            weight_in,
            bias_in,
            step_in,
            decay_in,
            skip_in,
            carried,
        )

    ignored_out, pullback = jax.vjp(
        full_mixer,
        padded,
        step_raw,
        conv_weight,
        conv_bias,
        step_bias,
        decay_log,
        skip_weight,
    )
    (
        grad_padded,
        grad_step_raw,
        grad_conv_weight,
        grad_conv_bias,
        grad_step_bias,
        grad_decay_log,
        grad_skip,
    ) = pullback((grad_mixed, next_grad))
    returned = passed_along(grad_padded[:width], -1)
    grad_rows = grad_padded[width:]
    grad_rows = jnp.concatenate([grad_rows[:-width], grad_rows[-width:] + returned])
    grad_late = jnp.concatenate([grad_rows, grad_step_raw], axis=1).astype(bf16)
    grad_all = jnp.concatenate([grad_gate, grad_late], axis=1)
    tensor_part = lax.dot_general(
        grad_all, full_weight, (((1,), (1,)), ((), ())), preferred_element_type=jnp.float32
    )
    mean_sum = jnp.sum(hidden * norm_gain[None, :] * tensor_part, axis=1)
    late_pad = -grad_late.shape[1] % 128
    late_weight = jnp.dot(
        normed.T,
        jnp.pad(grad_late, ((0, 0), (0, late_pad))),
        preferred_element_type=jnp.float32,
    ).astype(bf16)
    parts = (
        grad_conv_weight[:, :local_inner],
        grad_conv_bias[:local_inner],
        grad_step_bias,
        grad_decay_log,
        grad_skip,
        grad_gain_gate,
        grad_conv_weight[:, local_inner:],
        grad_conv_bias[local_inner:],
    )
    part_rows = -(-sum(p.size for p in parts) // 2048) * 16
    own_grad, mean_sum, late_grads, smalls = exchange(
        [
            (tensor_part.astype(bf16), ("tp",), 1),
            (mean_sum.reshape(tokens // 128, 128), ("tp",), None),
            (late_weight, everyone, 0),
            (flat_rows(parts, part_rows), everyone, None),
        ],
        2,
    )
    mean_term = mean_sum.reshape(tokens, 1) / MODEL_WIDTH
    own_cotangent = lax.dynamic_slice_in_dim(output_cotangent, column, share, 1).astype(jnp.float32)
    own_gain = lax.dynamic_slice_in_dim(norm_gain, column, share, 0)
    input_grad = (
        own_cotangent
        + inv_rms * own_grad * own_gain[None, :]
        - own_hidden * inv_rms**3 * mean_term
    )
    grad_gain_norm = jnp.sum(own_grad * own_hidden * inv_rms, axis=0)
    smalls = smalls.reshape(-1)
    split = []
    at = 0
    for p in parts:
        split.append(smalls[at : at + p.size])
        at += p.size
    state_part = late_grads[:, local_inner : local_inner + 2 * STATE].astype(bf16)
    state_grad, conv_shared, gain_norm = exchange(
        [
            (state_part, ("tp",), None),
            (flat_rows([split[6], split[7]], 16), ("tp",), None),
            (flat_rows([grad_gain_norm], 8), everyone, None),
        ],
        3,
    )
    conv_shared = conv_shared.reshape(-1)
    conv_state = conv_shared[: KCONV * 2 * STATE].reshape(KCONV, 2 * STATE)
    bias_state = conv_shared[KCONV * 2 * STATE : (KCONV + 1) * 2 * STATE]
    return (
        block_output,
        input_grad,
        gain_norm.reshape(-1)[:share],
        gate_grad,
        late_grads[:, :local_inner],
        late_grads[:, local_inner + 2 * STATE : local_inner + 2 * STATE + heads],
        state_grad,
        split[0].reshape(KCONV, local_inner),
        split[1],
        conv_state,
        bias_state,
        split[2],
        split[3],
        split[4],
        split[5],
        out_proj_grad,
    )


def solution(mesh):
    return jax.shard_map(
        on_device,
        mesh=mesh,
        in_specs=(
            P(("dp", "ctx"), None),
            P(("dp", "ctx")),
            P(),
            P(("dp", "ctx"), "tp"),
            P(("dp", "ctx"), "tp"),
            P(("dp", "ctx"), "tp"),
            P(("dp", "ctx"), None),
            P(None, "tp"),
            P("tp"),
            P(),
            P(),
            P("tp"),
            P("tp"),
            P("tp"),
            P("tp"),
            P("tp", ("dp", "ctx")),
            P(("dp", "ctx"), None),
        ),
        out_specs=(
            P(("dp", "ctx"), "tp"),
            P(("dp", "ctx"), "tp"),
            P("tp"),
            P(("dp", "ctx"), "tp"),
            P(("dp", "ctx"), "tp"),
            P(("dp", "ctx"), "tp"),
            P(("dp", "ctx"), None),
            P(None, "tp"),
            P("tp"),
            P(),
            P(),
            P("tp"),
            P("tp"),
            P("tp"),
            P("tp"),
            P("tp", ("dp", "ctx")),
        ),
        check_vma=False,
    )
```

```python
import jax
import jax.numpy as jnp
from jax import lax
from jax.experimental import pallas as pl
from jax.experimental.pallas import tpu as pltpu
from jax.sharding import PartitionSpec as P

MODEL_WIDTH = 1024
HEADDIM = 64
STATE = 128
KCONV = 4
SPAN = 256
INNER = 2048


EPSILON = 1e-05
HIGHEST = lax.Precision.HIGHEST


def passed_along(block, distance):
    devices = range(lax.axis_size("ctx"))
    route = [(i - distance, i) for i in devices if i - distance in devices]
    return lax.ppermute(block, "ctx", route)


def place_in(axes):
    place = lax.axis_index(axes[0])
    for axis in axes[1:]:
        place = place * lax.axis_size(axis) + lax.axis_index(axis)
    return place


def device_at(axes, place):
    if len(axes) == 1:
        return {axes[0]: place}
    inner = lax.axis_size(axes[1])
    return {axes[0]: place // inner, axes[1]: lax.rem(place, inner)}


def exchange_kernel(plans, *refs):
    count = len(plans)
    inputs, outputs = refs[:count], refs[count : 2 * count]
    scratch = refs[2 * count :]
    greeted = []
    for axes, size, _, _, _ in plans:
        if axes not in greeted:
            greeted.append(axes)
    barrier = pltpu.get_barrier_semaphore()
    expected = 0
    for axes in greeted:
        size = [p[1] for p in plans if p[0] == axes][0]
        me = place_in(axes)
        for off in range(1, size):
            pl.semaphore_signal(
                barrier,
                inc=1,
                device_id=device_at(axes, lax.rem(me + off, size)),
                device_id_type=pl.DeviceIdType.MESH,
            )
        expected += size - 1
    pl.semaphore_wait(barrier, expected)
    copies = []
    for index, (axes, size, dim, block, first) in enumerate(plans):
        received, own, send_sem, recv_sem, own_sem = scratch[5 * index : 5 * index + 5]
        x = inputs[index]
        me = place_in(axes)

        def piece(place, x=x, dim=dim, block=block, first=first):
            if dim is None:
                return x
            start = pl.multiple_of(place * block[dim], block[dim])
            if dim == 0:
                return x.at[pl.ds(start, block[0]), pl.ds(first, block[1])]
            return x.at[:, pl.ds(start, block[1])]

        sends = []
        for off in range(size - 1, 0, -1):
            target = lax.rem(me + off, size)
            copy = pltpu.make_async_remote_copy(
                src_ref=piece(target),
                dst_ref=received.at[off - 1],
                send_sem=send_sem.at[off - 1],
                recv_sem=recv_sem.at[off - 1],
                device_id=device_at(axes, target),
                device_id_type=pl.DeviceIdType.MESH,
            )
            copy.start()
            sends.append(copy)
        local = pltpu.make_async_copy(piece(me), own, own_sem)
        local.start()
        copies.append((sends, local))
    for index in reversed(range(count)):
        _, size, _, block, _ = plans[index]
        received, own = scratch[5 * index : 5 * index + 2]
        sends, local = copies[index]
        local.wait()
        for copy in sends:
            copy.wait_recv()
        rows = min(16, block[0])

        def add(step, carry, received=received, own=own, out=outputs[index], size=size, rows=rows):
            at = pl.ds(pl.multiple_of(step * rows, rows), rows)
            total = own[at, :].astype(jnp.float32)
            for k in range(size - 1):
                total = total + received[k, at, :].astype(jnp.float32)
            out[at, :] = total.astype(out.dtype)
            return carry

        lax.fori_loop(0, block[0] // rows, add, 0)
    for sends, _ in copies:
        for copy in sends:
            copy.wait_send()


def exchange(items, collective_id):
    plans, out_shape, scratch = [], [], []
    for x, axes, dim, *more in items:
        size = 1
        for axis in axes:
            size *= lax.axis_size(axis)
        block = list(x.shape)
        if dim is not None:
            block[dim] //= size
        first = 0
        if more:
            first, block[1] = more[0]
        block = tuple(block)
        plans.append((axes, size, dim, block, first))
        out_shape.append(jax.ShapeDtypeStruct(block, more[1] if more else jnp.float32))
        scratch += [
            pltpu.VMEM((size - 1,) + block, x.dtype),
            pltpu.VMEM(block, x.dtype),
            pltpu.SemaphoreType.DMA((size - 1,)),
            pltpu.SemaphoreType.DMA((size - 1,)),
            pltpu.SemaphoreType.DMA,
        ]
    return pl.pallas_call(
        lambda *refs: exchange_kernel(plans, *refs),
        out_shape=tuple(out_shape),
        in_specs=[pl.BlockSpec(memory_space=pl.ANY)] * len(items),
        out_specs=tuple([pl.BlockSpec(memory_space=pltpu.VMEM)] * len(items)),
        scratch_shapes=scratch,
        compiler_params=pltpu.CompilerParams(collective_id=collective_id, has_side_effects=True),
        name="exchange" + str(collective_id),
    )(*[item[0] for item in items])


def flat_rows(parts, rows):
    flat = jnp.concatenate([p.reshape(-1) for p in parts])
    return jnp.pad(flat, (0, rows * 128 - flat.shape[0])).reshape(rows, 128)


def conv_apply(padded, flags_padded, conv_weight, conv_bias):
    width = KCONV - 1
    count = padded.shape[0] - width
    segments = jnp.cumsum(flags_padded)
    own = segments[width:]
    result = jnp.zeros((count, padded.shape[1]), jnp.float32) + conv_bias[None, :]
    for lag in range(KCONV):
        valid = (segments[width - lag : width - lag + count] == own).astype(jnp.float32)
        result = (
            result
            + conv_weight[lag][None, :] * padded[width - lag : width - lag + count] * valid[:, None]
        )
    return result


def span_parts(inner_values, step_size, state_in, state_out, sequence_starts, decay_rate):
    count = inner_values.shape[0]
    heads = step_size.shape[1]
    spans = count // SPAN
    log_decay = (step_size * decay_rate[None, :]).reshape(spans, SPAN, heads)
    ones_below = jnp.tril(jnp.ones((SPAN, SPAN), jnp.float32))
    cumulative = jnp.einsum("ts,ksh->kth", ones_below, log_decay, precision=HIGHEST)
    segments = jnp.cumsum(sequence_starts.reshape(spans, SPAN), axis=1)
    block_values = inner_values.reshape(spans, SPAN, heads, HEADDIM)
    block_step = step_size.reshape(spans, SPAN, heads)
    block_in = state_in.reshape(spans, SPAN, STATE)
    block_out = state_out.reshape(spans, SPAN, STATE)
    order = jnp.arange(SPAN)
    lower = order[:, None] >= order[None, :]
    same = ((segments[:, :, None] == segments[:, None, :]) & lower[None])[..., None]
    spread = cumulative[:, :, None, :] - cumulative[:, None, :, :]
    decay = jnp.where(same, jnp.exp(jnp.where(same, spread, 0.0)), 0.0)
    scores = jnp.einsum("ktn,ksn->kts", block_out, block_in)
    mixing = decay * scores[..., None] * block_step[:, None, :, :]
    inner_mixed = jnp.einsum("ktsh,kshp->kthp", mixing, block_values)
    ending = (segments == segments[:, -1:])[..., None]
    to_end = jnp.where(ending, jnp.exp(cumulative[:, -1:, :] - cumulative), 0.0) * block_step
    states = jnp.einsum(
        "kshp,ksn->khpn", block_values * to_end[..., None], block_in
    )
    passing = jnp.where((segments == 0)[..., None], jnp.exp(cumulative), 0.0)
    return (inner_mixed, states, passing)


def fold_spans(states, passing):
    ends = passing[:, -1, :]
    state = jnp.zeros(states.shape[1:], jnp.float32)
    product = jnp.ones(ends.shape[1:], jnp.float32)
    span_states, span_decays = [], []
    for k in range(states.shape[0]):
        span_states.append(state)
        span_decays.append(product)
        state = ends[k][:, None, None] * state + states[k]
        product = ends[k] * product
    return (jnp.stack(span_states), jnp.stack(span_decays), state, product)


def mixer_front(
    padded, flags_padded, sequence_starts, step_raw, conv_weight, conv_bias, step_bias, decay_log
):
    inner_width = padded.shape[1] - 2 * STATE
    activated = jax.nn.silu(conv_apply(padded, flags_padded, conv_weight, conv_bias))
    inner_values = activated[:, :inner_width]
    state_in = activated[:, inner_width : inner_width + STATE]
    state_out = activated[:, inner_width + STATE :]
    step_size = jax.nn.softplus(step_raw + step_bias[None, :])
    decay_rate = -jnp.exp(decay_log)
    inner_mixed, states, passing = span_parts(
        inner_values, step_size, state_in, state_out, sequence_starts, decay_rate
    )
    span_states, span_decays, final_state, final_product = fold_spans(states, passing)
    kept = (inner_values, state_out, inner_mixed, passing, span_states, span_decays)
    return (kept, final_state, final_product)


def finish(kept, carried, skip):
    inner_values, state_out, inner_mixed, passing, span_states, span_decays = kept
    spans = inner_mixed.shape[0]
    heads = inner_mixed.shape[2]
    initial = span_states + span_decays[:, :, None, None] * carried[None]
    block_out = state_out.reshape(spans, SPAN, STATE)
    from_state = jnp.einsum("ktn,khpn->kthp", block_out, initial)
    block_values = inner_values.reshape(spans, SPAN, heads, HEADDIM)
    total = inner_mixed + passing[..., None] * from_state + skip[None, None, :, None] * block_values
    return total.reshape(inner_values.shape[0], heads * HEADDIM)


def mixer(
    padded,
    flags_padded,
    sequence_starts,
    step_raw,
    conv_weight,
    conv_bias,
    step_bias,
    decay_log,
    skip,
    carried,
):
    kept, final_state, final_product = mixer_front(
        padded,
        flags_padded,
        sequence_starts,
        step_raw,
        conv_weight,
        conv_bias,
        step_bias,
        decay_log,
    )
    output = finish(kept, carried, skip)
    return (output, final_state + final_product[:, None, None] * carried)


def on_device(
    block_input_activations,
    sequence_first_token,
    norm_gain,
    gate_proj,
    input_proj,
    step_proj,
    state_proj,
    conv_inner_weight,
    conv_inner_bias,
    conv_state_weight,
    conv_state_bias,
    step_bias,
    decay_log,
    skip_weight,
    gate_gain,
    out_proj,
    output_cotangent,
):
    everyone = ("dp", "ctx")
    bf16 = jnp.bfloat16
    local_inner = gate_proj.shape[1]
    heads = step_bias.shape[0]
    width = KCONV - 1
    full_weight = lax.all_gather(
        jnp.concatenate([gate_proj, input_proj, state_proj, step_proj], axis=1),
        everyone,
        axis=0,
        tiled=True,
    )
    full_out_t = lax.all_gather(out_proj.T, everyone, axis=0, tiled=True)
    hidden = block_input_activations.astype(jnp.float32)
    inv_rms = lax.rsqrt(jnp.mean(hidden * hidden, axis=1, keepdims=True) + EPSILON)
    normed = (hidden * inv_rms * norm_gain[None, :]).astype(bf16)
    projected = jnp.dot(normed, full_weight, preferred_element_type=jnp.float32)
    step_raw = projected[:, 2 * local_inner + 2 * STATE :]
    gate = projected[:, :local_inner]
    conv_rows = projected[:, local_inner : 2 * local_inner + 2 * STATE].astype(bf16)
    sequence_starts = sequence_first_token.astype(jnp.float32)
    tail_rows, tail_flags = passed_along(
        (conv_rows[-width:], sequence_starts[-width:].astype(bf16)), 1
    )
    padded = jnp.concatenate([tail_rows, conv_rows], axis=0).astype(jnp.float32)
    flags_padded = jnp.concatenate([tail_flags.astype(jnp.float32), sequence_starts])
    conv_weight = jnp.concatenate([conv_inner_weight, conv_state_weight], axis=1)
    conv_bias = jnp.concatenate([conv_inner_bias, conv_state_bias])
    kept, final_state, final_product = mixer_front(
        padded,
        flags_padded,
        sequence_starts,
        step_raw,
        conv_weight,
        conv_bias,
        step_bias,
        decay_log,
    )
    carried = passed_along(final_state, 1)
    mixed = finish(kept, carried, skip_weight)
    gate_silu = jax.nn.silu(gate)
    gated = mixed * gate_silu
    grad_gated_normed = jnp.dot(output_cotangent, full_out_t, preferred_element_type=jnp.float32)
    scaled = grad_gated_normed * gate_gain[None, :]
    tokens = hidden.shape[0]
    (row_sums,) = exchange(
        [
            (
                flat_rows(
                    [jnp.sum(gated * gated, axis=1), jnp.sum(gated * scaled, axis=1)],
                    2 * tokens // 128,
                ),
                ("tp",),
                None,
            )
        ],
        1,
    )
    row_sums = row_sums.reshape(2, tokens)
    gate_inv = lax.rsqrt(row_sums[0] / INNER + EPSILON)[:, None]
    gated_normed = (gated * gate_inv * gate_gain[None, :]).astype(bf16)
    share = MODEL_WIDTH // lax.axis_size("tp")
    column = lax.axis_index("tp") * share
    branch_part = lax.dot_general(
        gated_normed, full_out_t, (((1,), (1,)), ((), ())), preferred_element_type=jnp.float32
    ).astype(bf16)
    own_hidden = lax.dynamic_slice_in_dim(hidden, column, share, 1)
    grad_gated = gate_inv * scaled - gated * gate_inv**3 * (row_sums[1] / INNER)[:, None]
    grad_gain_gate = jnp.sum(grad_gated_normed * gated * gate_inv, axis=0)
    sigmoid_gate = jax.nn.sigmoid(gate)
    grad_mixed = grad_gated * gate_silu
    grad_gate = (
        grad_gated * mixed * sigmoid_gate * (1.0 + gate * (1.0 - sigmoid_gate))
    ).astype(bf16)
    grad_out = lax.dot_general(
        output_cotangent,
        gated_normed,
        (((0,), (0,)), ((), ())),
        preferred_element_type=jnp.float32,
    ).astype(bf16)
    grad_gate_weight = jnp.dot(
        normed.T, grad_gate, preferred_element_type=jnp.float32
    ).astype(bf16)
    first_part = jnp.concatenate([grad_gate_weight, grad_out], axis=1)
    grad_mixed, branch_part, first_part = lax.optimization_barrier(
        (grad_mixed, branch_part, first_part)
    )
    branch = lax.psum_scatter(branch_part, "tp", scatter_dimension=1, tiled=True)
    block_output = (own_hidden + branch.astype(jnp.float32)).astype(bf16)
    first_grads = lax.psum_scatter(
        first_part, everyone, scatter_dimension=0, tiled=True
    ).astype(jnp.float32)
    gate_grad = first_grads[:, :local_inner]
    out_proj_grad = first_grads[:, local_inner:].T

    def state_effect(carried_in):
        return finish(kept, carried_in, skip_weight)

    ignored, state_pull = jax.vjp(state_effect, carried)
    (through_mixed,) = state_pull(grad_mixed)
    next_grad = passed_along(through_mixed, -1)

    def full_mixer(padded_in, raw_in, weight_in, bias_in, step_in, decay_in, skip_in):
        return mixer(
            padded_in,
            flags_padded,
            sequence_starts,
            raw_in,
            weight_in,
            bias_in,
            step_in,
            decay_in,
            skip_in,
            carried,
        )

    ignored_out, pullback = jax.vjp(
        full_mixer,
        padded,
        step_raw,
        conv_weight,
        conv_bias,
        step_bias,
        decay_log,
        skip_weight,
    )
    (
        grad_padded,
        grad_step_raw,
        grad_conv_weight,
        grad_conv_bias,
        grad_step_bias,
        grad_decay_log,
        grad_skip,
    ) = pullback((grad_mixed, next_grad))
    returned = passed_along(grad_padded[:width], -1)
    grad_rows = grad_padded[width:]
    grad_rows = jnp.concatenate([grad_rows[:-width], grad_rows[-width:] + returned])
    grad_late = jnp.concatenate([grad_rows, grad_step_raw], axis=1).astype(bf16)
    grad_all = jnp.concatenate([grad_gate, grad_late], axis=1)
    tensor_part = lax.dot_general(
        grad_all, full_weight, (((1,), (1,)), ((), ())), preferred_element_type=jnp.float32
    )
    mean_sum = jnp.sum(hidden * norm_gain[None, :] * tensor_part, axis=1)
    late_pad = -grad_late.shape[1] % 128
    late_weight = jnp.dot(
        normed.T,
        jnp.pad(grad_late, ((0, 0), (0, late_pad))),
        preferred_element_type=jnp.float32,
    ).astype(bf16)
    per_head = jnp.concatenate([grad_step_bias, grad_decay_log, grad_skip])
    inner_rows = jnp.concatenate(
        [
            grad_conv_weight[:, :local_inner],
            grad_conv_bias[None, :local_inner],
            grad_gain_gate[None, :],
            jnp.pad(per_head, (0, local_inner - 3 * heads))[None, :],
            jnp.zeros((1, local_inner), jnp.float32),
        ]
    )
    state_rows = jnp.concatenate(
        [
            grad_conv_weight[:, local_inner:],
            grad_conv_bias[None, local_inner:],
            jnp.zeros((3, 2 * STATE), jnp.float32),
        ]
    )
    wide = late_weight.shape[1] - local_inner - 2 * STATE
    own_grad, mean_sum, input_grads, state_part, step_grads, inner_rows, state_rows = exchange(
        [
            (tensor_part.astype(bf16), ("tp",), 1),
            (mean_sum.reshape(tokens // 128, 128), ("tp",), None),
            (late_weight, everyone, 0, (0, local_inner), jnp.float32),
            (late_weight, everyone, 0, (local_inner, 2 * STATE), bf16),
            (late_weight, everyone, 0, (local_inner + 2 * STATE, wide), jnp.float32),
            (inner_rows, everyone, None),
            (state_rows, everyone, None),
        ],
        2,
    )
    mean_term = mean_sum.reshape(tokens, 1) / MODEL_WIDTH
    own_cotangent = lax.dynamic_slice_in_dim(output_cotangent, column, share, 1).astype(jnp.float32)
    own_gain = lax.dynamic_slice_in_dim(norm_gain, column, share, 0)
    input_grad = (
        own_cotangent
        + inv_rms * own_grad * own_gain[None, :]
        - own_hidden * inv_rms**3 * mean_term
    )
    grad_gain_norm = jnp.sum(own_grad * own_hidden * inv_rms, axis=0)
    gain_rows = jnp.pad(grad_gain_norm[None, :], ((0, 7), (0, 0)))
    state_grad, state_rows, gain_rows = exchange(
        [
            (state_part, ("tp",), None),
            (state_rows, ("tp",), None),
            (gain_rows, everyone, None),
        ],
        3,
    )
    return (
        block_output,
        input_grad,
        gain_rows[0],
        gate_grad,
        input_grads,
        step_grads[:, :heads],
        state_grad,
        inner_rows[:KCONV],
        inner_rows[KCONV],
        state_rows[:KCONV],
        state_rows[KCONV],
        inner_rows[KCONV + 2, :heads],
        inner_rows[KCONV + 2, heads : 2 * heads],
        inner_rows[KCONV + 2, 2 * heads : 3 * heads],
        inner_rows[KCONV + 1],
        out_proj_grad,
    )


def solution(mesh):
    return jax.shard_map(
        on_device,
        mesh=mesh,
        in_specs=(
            P(("dp", "ctx"), None),
            P(("dp", "ctx")),
            P(),
            P(("dp", "ctx"), "tp"),
            P(("dp", "ctx"), "tp"),
            P(("dp", "ctx"), "tp"),
            P(("dp", "ctx"), None),
            P(None, "tp"),
            P("tp"),
            P(),
            P(),
            P("tp"),
            P("tp"),
            P("tp"),
            P("tp"),
            P("tp", ("dp", "ctx")),
            P(("dp", "ctx"), None),
        ),
        out_specs=(
            P(("dp", "ctx"), "tp"),
            P(("dp", "ctx"), "tp"),
            P("tp"),
            P(("dp", "ctx"), "tp"),
            P(("dp", "ctx"), "tp"),
            P(("dp", "ctx"), "tp"),
            P(("dp", "ctx"), None),
            P(None, "tp"),
            P("tp"),
            P(),
            P(),
            P("tp"),
            P("tp"),
            P("tp"),
            P("tp"),
            P("tp", ("dp", "ctx")),
        ),
        check_vma=False,
    )
```
